32 devices in a mesh: dp: 8 (over y, x, core), chan: 4 (over z).
Axes of the slice: x: 2, y: 2, z: 4, core: 2. Of those that a mesh axis runs over, the one named last changes fastest.
Arguments:
- pixels: bfloat16 [768, 512], P('dp', 'chan'), may hold values from -6 to 6
- embed_weight: bfloat16 [32, 16, 1024], P('chan'), may hold values from -1.5 to 1.5
- channel_bias: bfloat16 [32, 1024], P('chan'), may hold values from -3 to 3
- agg_query: bfloat16 [4, 1024], P('chan'), may hold values from -0.375 to 0.375
- key_weight: bfloat16 [1024, 256], P(None, 'chan'), may hold values from -0.1875 to 0.1875
- value_weight: bfloat16 [1024, 256], P(None, 'chan'), may hold values from -0.1875 to 0.1875
- final_query: bfloat16 [4, 64], P('chan'), may hold values from -10 to 10
- out_weight: bfloat16 [256, 1024], P('chan'), may hold values from -0.375 to 0.375
- group_counts: int32 [4], P('chan'), may hold values from 4 to 8, as said below
- grad_output: bfloat16 [768, 1024], P('dp'), may hold values from -0.21875 to 0.21875
Outputs:
- layer_out: bfloat16 [768, 1024], P('dp')
- grad_embed: float32 [32, 16, 1024], P('chan')
- grad_bias: float32 [32, 1024], P('chan')
- grad_agg: float32 [4, 1024], P('chan')
- grad_key: float32 [1024, 256], P(None, 'chan')
- grad_value: float32 [1024, 256], P(None, 'chan')
- grad_query: float32 [4, 64], P('chan')
- grad_out: float32 [256, 1024], P('chan')
The draws below stay inside these ranges and needn't reach their ends.
Inputs may be any that keep to these rules, and one draw needn't show every extreme that they name: A group's first group_counts[g] channels are live; some group has all 8 live.
All inputs are finite; a program needn't handle non-finite values.
Results may differ from the reference program's by a relative error of at most 0.018.
The reference program's roundings to bfloat16 on the way count: a program that leaves them out, or rounds other values in their place, can miss the bound.
Values may be sent and summed in bfloat16 or wider, within the bound.
No kernel may reach another device: no remote copies, remote signals or barrier semaphores. Data moves between devices by JAX's collectives and lax.ppermute only.
A program may use at most 64 MiB of HBM per device.

```python
import math
import jax
import jax.numpy as jnp
from jax import lax

D = 1024
PP = 16
CH_DEV = 8
HD = 64
TOK_DEV = 96
GROUPS = 4
HEADS = 4
CHANNELS = 32
TOKENS = 768
N_DP = 8


def draw_group_counts(key, part):
    first_key, second_key = jax.random.split(jax.random.fold_in(key, 17))
    counts = jax.random.randint(first_key, (GROUPS,), CH_DEV // 2, CH_DEV + 1)
    chosen = jax.random.randint(second_key, (), 0, GROUPS)
    return jnp.where(jnp.arange(GROUPS) == chosen, CH_DEV, counts).astype(jnp.int32)


def shard_levels(key, extent, cuts, low, top_value):
    def one(axis_at, blocks):
        heights = jax.random.uniform(jax.random.fold_in(jax.random.fold_in(key, 6), axis_at), (blocks,), jnp.float32, low / len(cuts), top_value / len(cuts))
        return jnp.repeat(jnp.exp(heights), extent[axis_at] // blocks).reshape((-1,) + (1,) * (len(extent) - axis_at - 1))

    loudness = one(*cuts[0])
    for cut in cuts[1:]:
        loudness = loudness * one(*cut)
    return loudness


def centred(rng, shape, width, most, cuts=(), kind=jnp.bfloat16):
    drawn = jax.random.normal(rng, shape, jnp.float32) * width
    if len(cuts) > 0:
        drawn = shard_levels(rng, shape, cuts, -0.22, 0.18) * drawn
    return jnp.clip(drawn, min=-most, max=most).astype(kind)


def setup_inputs(seed: int = 0) -> dict:
    key_of = jax.random.split(jax.random.key(seed), 11)
    pixels = centred(key_of[0], (TOKENS, CHANNELS * PP), 1.0, 6.0, ((0, 8), (1, 4)))
    embed_weight = centred(key_of[1], (CHANNELS, PP, D), PP ** -0.5, 1.5, ((0, 4),))
    channel_bias = centred(key_of[2], (CHANNELS, D), 0.5, 3.0, ((0, 4),))
    agg_query = centred(key_of[3], (GROUPS, D), (D // 4) ** -0.5, 0.375, ((0, 4),))
    key_weight = centred(key_of[4], (D, HEADS * HD), D ** -0.5, 0.1875, ((1, 4),))
    value_weight = centred(key_of[5], (D, HEADS * HD), D ** -0.5, 0.1875, ((1, 4),))
    final_query = centred(key_of[6], (HEADS, HD), 2.0, 10.0, ((0, 4),))
    out_weight = centred(key_of[7], (HEADS * HD, D), (HEADS * HD) ** -0.5, 0.375, ((0, 4),))
    group_counts = draw_group_counts(jax.random.fold_in(key_of[10], 71), 0)
    grad_output = centred(key_of[9], (TOKENS, D), TOKENS ** -0.5, 0.21875, ((0, 8),))
    return dict(pixels=pixels, embed_weight=embed_weight, channel_bias=channel_bias, agg_query=agg_query, key_weight=key_weight, value_weight=value_weight, final_query=final_query, out_weight=out_weight, group_counts=group_counts, grad_output=grad_output)


softcap = 15.0

def rounded(value):
    return lax.optimization_barrier(value.astype(jnp.bfloat16)).astype(jnp.float32)

def block_pass(pixel_rows, grad_rows, embed_weight, channel_bias, agg_query, key_weight, value_weight, final_query, out_weight, live_mask):
    tok_rows = pixel_rows.shape[0]
    patches = pixel_rows.reshape(tok_rows, CHANNELS, PP).astype(jnp.float32)
    embed_wide = rounded(jnp.einsum('tcp,cpd->tcd', patches, embed_weight.astype(jnp.float32)) + channel_bias.astype(jnp.float32)[None])
    query_rows = jnp.repeat(agg_query.astype(jnp.float32), CH_DEV, axis=0)
    agg_capped = softcap * jnp.tanh(jnp.einsum('tcd,cd->tc', embed_wide, query_rows) / softcap)
    agg_exp = jnp.exp(agg_capped) * live_mask[None]
    agg_total = agg_exp.reshape(tok_rows, GROUPS, CH_DEV).sum(-1)
    agg_weight = agg_exp / jnp.repeat(agg_total, CH_DEV, axis=1)
    agg_round = rounded(agg_weight)
    embed_four = embed_wide.reshape(tok_rows, GROUPS, CH_DEV, D)
    group_token = rounded(jnp.einsum('tgc,tgcd->tgd', agg_round.reshape(tok_rows, GROUPS, CH_DEV), embed_four))
    key_three = key_weight.astype(jnp.float32).reshape(D, HEADS, HD)
    value_three = value_weight.astype(jnp.float32).reshape(D, HEADS, HD)
    query_heads = final_query.astype(jnp.float32)
    keys = rounded(jnp.einsum('tgd,dhk->tghk', group_token, key_three))
    values = rounded(jnp.einsum('tgd,dhk->tghk', group_token, value_three))
    head_capped = softcap * jnp.tanh(jnp.einsum('tghk,hk->thg', keys, query_heads) / math.sqrt(HD) / softcap)
    head_exp = jnp.exp(head_capped)
    head_prob = head_exp / head_exp.sum(-1, keepdims=True)
    head_round = rounded(head_prob)
    attended = rounded(jnp.einsum('thg,tghk->thk', head_round, values))
    out_three = out_weight.astype(jnp.float32).reshape(HEADS, HD, D)
    layer_rows = jnp.einsum('thk,hkd->td', attended, out_three).astype(jnp.bfloat16)
    grad_wide = grad_rows.astype(jnp.float32)
    grad_out = jnp.einsum('thk,td->hkd', attended, grad_wide).reshape(HEADS * HD, D)
    attended_grad = rounded(jnp.einsum('td,hkd->thk', grad_wide, out_three))
    prob_grad = jnp.einsum('thk,tghk->thg', attended_grad, values)
    value_grad = rounded(jnp.einsum('thg,thk->tghk', head_round, attended_grad))
    score_grad = head_prob * (prob_grad - lax.optimization_barrier(jnp.sum(head_prob * prob_grad, -1, keepdims=True)))
    raw_grad = score_grad * (1.0 - (head_capped / softcap) ** 2) / math.sqrt(HD)
    key_grad = rounded(jnp.einsum('thg,hk->tghk', raw_grad, query_heads))
    grad_query = jnp.einsum('thg,tghk->hk', raw_grad, keys)
    grad_key = jnp.einsum('tgd,tghk->dhk', group_token, key_grad).reshape(D, HEADS * HD)
    grad_value = jnp.einsum('tgd,tghk->dhk', group_token, value_grad).reshape(D, HEADS * HD)
    head_parts = rounded(jnp.einsum('tghk,dhk->tghd', key_grad, key_three) + jnp.einsum('tghk,dhk->tghd', value_grad, value_three))
    token_grad = head_parts.sum(2)
    mix_grad = jnp.einsum('tgd,tgcd->tgc', token_grad, embed_four).reshape(tok_rows, CHANNELS)
    mix_weighted = (agg_weight * mix_grad).reshape(tok_rows, GROUPS, CH_DEV).sum(-1)
    agg_raw_grad = agg_weight * (mix_grad - jnp.repeat(mix_weighted, CH_DEV, axis=1)) * (1.0 - (agg_capped / softcap) ** 2)
    token_rep = jnp.repeat(token_grad, CH_DEV, axis=1)
    embed_grad = rounded(agg_round[..., None] * token_rep + agg_raw_grad[..., None] * query_rows[None])
    grad_agg = jnp.einsum('tc,tcd->cd', agg_raw_grad, embed_wide).reshape(GROUPS, CH_DEV, D).sum(1)
    grad_embed = jnp.einsum('tcp,tcd->cpd', patches, embed_grad)
    grad_bias = embed_grad.sum(0)
    return (layer_rows, (grad_embed, grad_bias, grad_agg, grad_key, grad_value, grad_query, grad_out))

def reference(pixels, embed_weight, channel_bias, agg_query, key_weight, value_weight, final_query, out_weight, group_counts, grad_output):
    live_mask = (jnp.arange(CHANNELS, dtype=jnp.int32) % CH_DEV < jnp.repeat(group_counts, CH_DEV)).astype(jnp.float32)
    pixel_blocks = pixels.reshape(N_DP, TOK_DEV, CHANNELS * PP)
    grad_blocks = grad_output.reshape(N_DP, TOK_DEV, D)
    zeros = (jnp.zeros((CHANNELS, PP, D), jnp.float32), jnp.zeros((CHANNELS, D), jnp.float32), jnp.zeros((GROUPS, D), jnp.float32), jnp.zeros((D, HEADS * HD), jnp.float32), jnp.zeros((D, HEADS * HD), jnp.float32), jnp.zeros((HEADS, HD), jnp.float32), jnp.zeros((HEADS * HD, D), jnp.float32))

    def advance(carry, inputs):
        layer_rows, grads = block_pass(inputs[0], inputs[1], embed_weight, channel_bias, agg_query, key_weight, value_weight, final_query, out_weight, live_mask)
        return (tuple((left + right for left, right in zip(carry, grads))), layer_rows)
    totals, layer = lax.scan(advance, zeros, (pixel_blocks, grad_blocks))
    return (layer.reshape(TOKENS, D), totals[0], totals[1], totals[2], totals[3], totals[4], totals[5], totals[6])
```

```python
import functools
import math

import jax
import jax.numpy as jnp
from jax import lax
from jax.experimental import pallas as pl
from jax.experimental.pallas import tpu as pltpu
from jax.sharding import PartitionSpec as P


softcap = 15.0
f32 = jnp.float32
bf16 = jnp.bfloat16


def dot_nn(a, b):
    return lax.dot_general(a, b, (((1,), (0,)), ((), ())), preferred_element_type=f32)


def dot_nt(a, b):
    return lax.dot_general(a, b, (((1,), (1,)), ((), ())), preferred_element_type=f32)


def dot_tn(a, b):
    return lax.dot_general(a, b, (((0,), (0,)), ((), ())), preferred_element_type=f32)


def split(x):
    hi = x.astype(bf16)
    return hi, (x - hi.astype(f32)).astype(bf16)


def expander(channels, width):
    rows = lax.broadcasted_iota(jnp.int32, (channels, width), 0)
    cols = lax.broadcasted_iota(jnp.int32, (channels, width), 1)
    return (cols // (width // channels) == rows).astype(f32)


def token_kernel(
    pix_ref, w_ref, b_ref, q_ref, cnt_ref, kt_ref, vt_ref, ow_ref, send_ref, xp_ref, ar_ref, aux_ref
):
    tok, channels = pix_ref.shape[0], b_ref.shape[0]
    width = pix_ref.shape[1]
    pix, w, b = pix_ref[...], w_ref[...], b_ref[...]
    q8 = jnp.broadcast_to(q_ref[...], (8, w.shape[1]))
    wq = dot_nt(q8, w)[0:1]
    bq = dot_nt(q8, b)[0:1]
    expand = expander(channels, width)
    hi, lo = split(expand * wq)
    logits = dot_nt(pix, hi) + dot_nt(pix, lo) + bq
    capped = softcap * jnp.tanh(logits / softcap)
    live = lax.broadcasted_iota(jnp.int32, (1, channels), 1) < cnt_ref[0]
    weight = jnp.exp(capped) * live.astype(f32)
    weight = weight / jnp.sum(weight, -1, keepdims=True)
    rounded = weight.astype(bf16)
    scaled = dot_nn(rounded, expand.astype(bf16)) * pix.astype(f32)
    x_hi, x_lo = split(scaled)
    token = dot_nn(x_hi, w) + dot_nn(x_lo, w) + dot_nn(rounded, b)
    send_ref[0:tok] = token.astype(bf16)
    extra = send_ref.shape[0] - tok
    head = kt_ref.shape[0]
    first = lax.axis_index("dp") * extra
    rows = lax.broadcasted_iota(jnp.int32, (extra, head), 0) + first
    cols = lax.broadcasted_iota(jnp.int32, (extra, head), 1)
    picked = dot_nn((rows == cols).astype(bf16), kt_ref[...])
    picked += dot_nn((rows == cols + head).astype(bf16), vt_ref[...])
    picked += dot_nn((rows == cols + 2 * head).astype(bf16), ow_ref[...])
    send_ref[tok:] = picked.astype(bf16)
    xp_ref[...] = x_hi
    ar_ref[...] = rounded
    aux_ref[0] = weight
    aux_ref[1] = capped


def attention_kernel(groups, gath_ref, kt_ref, vt_ref, fq_ref, ow_ref, go_ref, *out_refs):
    tok = go_ref.shape[0]
    head = kt_ref.shape[0]
    me = lax.axis_index("chan")
    kt, vt = kt_ref[...], vt_ref[...]
    fq = fq_ref[...]
    fq_wide = jnp.broadcast_to(fq, (128, head))
    scale = 1.0 / math.sqrt(head)
    keys, values, capped, exps = [], [], [], []
    for k in range(groups):
        g = lax.rem(me + k, groups)
        token = gath_ref[g, 0:tok, :]
        key = dot_nt(token, kt).astype(bf16)
        keys.append(key)
        values.append(dot_nt(token, vt).astype(bf16).astype(f32))
        cap = softcap * jnp.tanh(dot_nt(key, fq_wide) * scale / softcap)
        capped.append(cap)
        exps.append(jnp.exp(cap))
    inv = 1.0 / functools.reduce(jnp.add, exps)
    probs = [e * inv for e in exps]
    rounded = [p.astype(bf16).astype(f32) for p in probs]
    attended = functools.reduce(jnp.add, [r[:, :head] * v for r, v in zip(rounded, values)])
    attended = attended.astype(bf16)
    half = tok // 2
    packed = jnp.concatenate([attended[:half].astype(f32), attended[half:].astype(f32)], axis=1)
    packed = packed.astype(bf16)
    agrad = dot_nt(go_ref[...], ow_ref[...]).astype(bf16).astype(f32)
    pgrad = [
        jnp.broadcast_to(jnp.sum(agrad * v, -1, keepdims=True), (tok, 128)) for v in values
    ]
    mean = functools.reduce(jnp.add, [p * g for p, g in zip(probs, pgrad)])
    gq = jnp.zeros((1, head), f32)
    for k in range(groups):
        raw = probs[k] * (pgrad[k] - mean) * (1.0 - (capped[k] / softcap) ** 2) * scale
        raw = raw[:, :head]
        key_grad = raw * fq.astype(f32)
        value_grad = rounded[k][:, :head] * agrad
        gq += jnp.sum(raw * keys[k].astype(f32), 0, keepdims=True)
        out_refs[k][0:tok] = jnp.concatenate([key_grad, value_grad], axis=1).astype(bf16)
        out_refs[k][tok:] = packed
    out_refs[groups][...] = gq


def unpack(chunk, tok, head):
    low = chunk[tok:].astype(f32)
    return jnp.concatenate([low[:, :head], low[:, head:]], axis=0).astype(bf16)


def weight_kernel(groups, head, gath_ref, go_ref, *refs):
    chunk_refs, out_ref = refs[:-1], refs[-1]
    tok = go_ref.shape[0]
    me = lax.axis_index("chan")
    core = lax.axis_index("dp") % 2
    both = jnp.zeros((2 * head, gath_ref.shape[2]), f32)
    for k in range(groups):
        g = lax.rem(me + k, groups)
        both += dot_tn(chunk_refs[k][0:tok, :], gath_ref[g, 0:tok, :])
    attended = unpack(chunk_refs[0][...], tok, head)
    grad_out = dot_tn(attended, go_ref[...])
    full = jnp.concatenate([both, grad_out], axis=0).astype(bf16)
    panels = out_ref.shape[1]
    for i in range(panels):
        out_ref[core, i] = full[:, i * 128 : (i + 1) * 128]
        out_ref[1 - core, i] = full[:, (i + panels) * 128 : (i + panels + 1) * 128]


def embed_kernel(
    groups, head, pix_ref, w_ref, b_ref, xp_ref, ar_ref, aux_ref, gq_ref, all_ref, *refs
):
    chunk_refs, out_ref = refs[:-1], refs[-1]
    tok, width = pix_ref.shape
    channels = b_ref.shape[0]
    me = lax.axis_index("chan")
    core = lax.axis_index("dp") % 2
    xp, ar = xp_ref[...], ar_ref[...]
    tgrad = jnp.zeros((tok, w_ref.shape[1]), f32)
    halfrows = out_ref.shape[2]
    panels = []
    for k in range(groups):
        h = lax.rem(me + groups - k, groups)
        both = chunk_refs[k][0:tok, :]
        tgrad += dot_nn(both, all_ref[h, 0 : 2 * head, :]).astype(bf16).astype(f32)
        panels.append((h, jnp.concatenate([dot_tn(xp, both), dot_tn(ar, both)], axis=0)))
    pix = pix_ref[...].astype(f32)
    expand = expander(channels, width)
    hi, lo = split(tgrad)
    inner = (dot_nt(hi, w_ref[...]) + dot_nt(lo, w_ref[...])) * pix
    i_hi, i_lo = split(inner)
    e16 = expand.astype(bf16)
    mix = dot_nt(i_hi, e16) + dot_nt(i_lo, e16) + dot_nt(hi, b_ref[...]) + dot_nt(lo, b_ref[...])
    weight, capped = aux_ref[0], aux_ref[1]
    raw = weight * (mix - jnp.sum(weight * mix, -1, keepdims=True))
    raw = raw * (1.0 - (capped / softcap) ** 2)
    r_hi, r_lo = split(raw)
    s_pix = jnp.sum((dot_nn(r_hi, e16) + dot_nn(r_lo, e16)) * pix, 0, keepdims=True)
    s_chan = jnp.sum(raw, 0, keepdims=True)
    wide = 2 * head
    low = jnp.concatenate([s_pix, jnp.zeros((1, wide - width), f32)], axis=1) if width < wide else s_pix
    rest = jnp.concatenate(
        [s_chan, jnp.zeros((1, wide - channels - head), f32), gq_ref[...]], axis=1
    )
    tail_rows = 2 * halfrows - width - channels
    for h, panel in panels:
        tail = jnp.concatenate([low, rest, jnp.zeros((tail_rows - 2, wide), f32)], axis=0)
        full = jnp.concatenate([panel, tail], axis=0).astype(bf16).astype(f32)
        out_ref[core, h] = full[:halfrows].astype(bf16)
        out_ref[1 - core, h] = full[halfrows:].astype(bf16)


def layer_kernel(groups, head, tok, all_ref, *refs):
    chunk_refs, out_ref = refs[:-1], refs[-1]
    me = lax.axis_index("chan")
    acc = jnp.zeros(out_ref.shape, f32)
    for k in range(groups):
        h = lax.rem(me + groups - k, groups)
        acc += dot_nn(unpack(chunk_refs[k][...], tok, head), all_ref[h, 2 * head :, :])
    out_ref[...] = acc.astype(bf16)


def call(kernel, out_shape, args, smem=()):
    in_specs = [
        pl.BlockSpec(memory_space=pltpu.SMEM if i in smem else pltpu.VMEM) for i in range(len(args))
    ]
    return pl.pallas_call(
        kernel,
        out_shape=out_shape,
        in_specs=in_specs,
        out_specs=jax.tree.map(lambda _: pl.BlockSpec(memory_space=pltpu.VMEM), out_shape),
    )(*args)


def shaped(shape, dtype):
    return jax.ShapeDtypeStruct(shape, dtype)


def exchange(value, devices, flip):
    return lax.ppermute(value, "dp", [(j, j ^ flip(j)) for j in range(devices)])


def flips(devices):
    bits = list(range(1, devices.bit_length() - 1))
    return [
        lambda j, low=low, high=high: (1 << low) if j % 2 == 0 else (1 << high)
        for low, high in zip(bits, reversed(bits))
    ]


def add_rounded(a, b):
    return (a.astype(f32) + b.astype(f32)).astype(bf16)


def gather_rows(part, devices):
    n, s, d = part.shape
    index = lax.axis_index("dp")
    core = index % 2
    steps = devices.bit_length() - 2
    cur = part[:, None]
    for step, flip in enumerate(flips(devices)):
        got = exchange(cur, devices, flip)
        bit = jnp.where(core == 0, (index >> (1 + step)) & 1, (index >> (steps - step)) & 1)
        cur = jnp.where(bit == 0, jnp.stack([cur, got], 1), jnp.stack([got, cur], 1))
        cur = cur.reshape(n, -1, s, d)
    other = exchange(cur, devices, lambda j: 1)
    even = jnp.where(core == 0, cur, other)
    odd = jnp.where(core == 0, other, cur)
    odd = odd.reshape((n,) + (2,) * steps + (s, d))
    odd = odd.transpose((0,) + tuple(range(steps, 0, -1)) + (steps + 1, steps + 2))
    odd = odd.reshape(n, devices // 2, s, d)
    return jnp.stack([even, odd], 2).reshape(n, devices * s, d)


def per_device(
    devices,
    groups,
    pixels,
    embed_weight,
    channel_bias,
    agg_query,
    key_weight,
    value_weight,
    final_query,
    out_weight,
    group_counts,
    grad_output,
):
    tok, width = pixels.shape
    channels, pixel_count, model = embed_weight.shape
    head = key_weight.shape[1]
    w = embed_weight.reshape(channels * pixel_count, model)
    kt, vt = key_weight.T, value_weight.T
    share = 3 * head // devices
    send, xp, ar, aux = call(
        token_kernel,
        (
            shaped((tok + share, model), bf16),
            shaped((tok, width), bf16),
            shaped((tok, channels), bf16),
            shaped((2, tok, channels), f32),
        ),
        (pixels, w, channel_bias, agg_query, group_counts, kt, vt, out_weight),
        smem=(4,),
    )
    gathered = lax.all_gather(send, "chan", axis=0, tiled=False)
    chunk = shaped((tok + tok // 2, 2 * head), bf16)
    *chunks, gq = call(
        functools.partial(attention_kernel, groups),
        (chunk,) * groups + (shaped((1, head), f32),),
        (gathered, kt, vt, final_query, out_weight, grad_output),
    )
    received = [chunks[0]] + [
        lax.ppermute(chunks[k], "chan", [(j, (j + k) % groups) for j in range(groups)])
        for k in range(1, groups)
    ]
    every = gather_rows(gathered[:, tok:, :], devices)
    panels = model // 256
    early = call(
        functools.partial(weight_kernel, groups, head),
        shaped((2, panels, 3 * head, 128), bf16),
        (gathered, grad_output, *chunks),
    )
    rows = -(-(width + channels + 2) // 16) * 8
    late = call(
        functools.partial(embed_kernel, groups, head),
        shaped((2, groups, rows, 2 * head), bf16),
        (pixels, w, channel_bias, xp, ar, aux, gq, every, *received),
    )
    layer_out = call(
        functools.partial(layer_kernel, groups, head, tok),
        shaped((tok, model), bf16),
        (every, *received),
    )
    both = jnp.concatenate([early.reshape(2, -1, 128), late.reshape(2, -1, 128)], axis=1)
    total = add_rounded(both[0], exchange(both[1], devices, lambda j: 1))
    for flip in flips(devices):
        total = add_rounded(total, exchange(total, devices, flip))
    other = exchange(total, devices, lambda j: 1)
    core = lax.axis_index("dp") % 2
    low = jnp.where(core == 0, total, other).astype(f32)
    high = jnp.where(core == 0, other, total).astype(f32)
    cut = panels * 3 * head
    grads = jnp.concatenate([low[:cut], high[:cut]], axis=0)
    grads = grads.reshape(2 * panels, 3 * head, 128).transpose(1, 0, 2).reshape(3 * head, model)
    m = jnp.concatenate(
        [low[cut:].reshape(groups, rows, 128), high[cut:].reshape(groups, rows, 128)], axis=1
    )
    m = m.transpose(1, 0, 2).reshape(2 * rows, groups * 128)
    edge = width + channels
    s_pix = m[edge, :width]
    s_chan = m[edge + 1, :channels]
    gq = m[edge + 1, 2 * head - head : 2 * head][None]
    s_all = jnp.concatenate([s_pix, s_chan])
    proj = every[:, : 2 * head, :].reshape(groups * 2 * head, model)
    full = dot_nn(m[:edge].astype(bf16), proj) + s_all[:, None] * agg_query.astype(f32)
    grad_embed = full[:width].reshape(channels, pixel_count, model)
    grad_bias = full[width:]
    hi, lo = split(s_all[None])
    table = jnp.concatenate([w, channel_bias], axis=0)
    grad_agg = dot_nn(hi, table) + dot_nn(lo, table)
    return (
        layer_out,
        grad_embed,
        grad_bias,
        grad_agg,
        grads[:head].T,
        grads[head : 2 * head].T,
        gq,
        grads[2 * head :],
    )


def solution(mesh):
    return jax.shard_map(
        functools.partial(per_device, mesh.shape["dp"], mesh.shape["chan"]),
        mesh=mesh,
        in_specs=(
            P("dp", "chan"),
            P("chan", None, None),
            P("chan", None),
            P("chan", None),
            P(None, "chan"),
            P(None, "chan"),
            P("chan", None),
            P("chan", None),
            P("chan"),
            P("dp", None),
        ),
        out_specs=(
            P("dp", None),
            P("chan", None, None),
            P("chan", None),
            P("chan", None),
            P(None, "chan"),
            P(None, "chan"),
            P("chan", None),
            P("chan", None),
        ),
        check_vma=False,
    )
```
